256 devices in a mesh: ph: 4 (over x_lo, core), ka: 64 (over x_hi, z, y).
Axes of the slice: x: 4 (x_hi: 2, x_lo: 2; x = x_hi * 2 + x_lo), y: 4, z: 8, core: 2. Of those that a mesh axis runs over, the one named last changes fastest.
Arguments:
- g_wan: bfloat16 [256, 48, 48, 2, 1024], P('ka', 'ph'), may hold values from -6 to 6
- el_cells: int32 [3, 256], replicated, may hold values from -6 to 6
- ph_cells: int32 [3, 48], P(None, 'ph'), may hold values from -4 to 4
- q_point: int32 [3], replicated, may hold values from 0 to 63
- kpoints: int32 [3, 16384], P(None, 'ka'), may hold values from 0 to 63
- eigvec: float32 [2, 48, 48], replicated, may hold values from -0.875 to 0.875
- omega: float32 [48], replicated, may hold values from 0.25 to 4
Outputs:
- strength: float32 [48, 32, 16384], P('ph', None, 'ka')
The draws below stay inside these ranges and needn't reach their ends.
All inputs are finite; a program needn't handle non-finite values.
Results may differ from the reference program's by a relative error of at most 0.0018.
Values may be sent and summed in bfloat16 or wider, within the bound.
No kernel may reach another device: no remote copies, remote signals or barrier semaphores. Data moves between devices by JAX's collectives and lax.ppermute only.
A program may use at most 128 MiB of HBM per device.

```python
import math
import jax
import jax.numpy as jnp
from jax import lax

W = 32
NU = 48
KGRID = 64
K_DEV = 256
NRE = 256
NRP = 48
NK = 16384
N_KA = 64


def place_ends(array, key, low, high):
    dims = array.shape
    index_at = [jax.random.randint(jax.random.fold_in(key, axis), (), 0, dims[axis]) for axis in range(len(dims))]
    array = array.at[tuple(index_at)].set(low)
    longest = dims.index(max(dims))
    index_at[longest] = (index_at[longest] + 1) % dims[longest]
    return array.at[tuple(index_at)].set(high)


def shard_levels(key, dims, shards, low, high):
    loudness, own = 1.0, jax.random.fold_in(key, 6)
    for dim, parts in shards:
        heights = jnp.exp(jax.random.uniform(jax.random.fold_in(own, dim), (parts,), jnp.float32, low / len(shards), high / len(shards)))
        loudness = loudness * jnp.repeat(heights, dims[dim] // parts).reshape([-1 if axis == dim else 1 for axis in range(len(dims))])
    return loudness


def scatter_about(stream_key, extent, width, most, split=(), held_as=jnp.bfloat16):
    loudness = shard_levels(stream_key, extent, split, -0.22, 0.18) if split else 1.0
    result = jax.random.normal(stream_key, extent, jnp.float32) * width * loudness
    return jnp.minimum(jnp.maximum(result, -most), most).astype(held_as)


def setup_inputs(seed: int = 0) -> dict:
    arg_keys = jax.random.split(jax.random.key(seed), 8)
    return {
        "g_wan": scatter_about(arg_keys[0], (NRE, NRP, NU, 2, W * W), 1.0, 6.0, ((0, 64), (1, 4))),
        "el_cells": place_ends(jax.random.randint(arg_keys[1], (3, NRE), -6, 7), jax.random.fold_in(arg_keys[1], 1), -6, 6).astype(jnp.int32),
        "ph_cells": place_ends(jax.random.randint(arg_keys[2], (3, NRP), -4, 5), jax.random.fold_in(arg_keys[2], 1), -4, 4).astype(jnp.int32),
        "q_point": jax.random.randint(arg_keys[3], (3,), 0, KGRID).astype(jnp.int32),
        "kpoints": place_ends(jax.random.randint(arg_keys[4], (3, NK), 0, KGRID), jax.random.fold_in(arg_keys[4], 1), 0, KGRID - 1).astype(jnp.int32),
        "eigvec": scatter_about(arg_keys[5], (2, NU, NU), NU ** -0.5, 0.875, (), jnp.float32),
        "omega": jnp.clip(jnp.exp(jax.random.uniform(arg_keys[6], (NU,), jnp.float32, math.log(0.25), math.log(4.0))), 0.25, 4.0),
    }


def angles(numerators, vectors):
    summed = lax.optimization_barrier(jnp.sum(numerators[:, :, None] * vectors[:, None, :], axis=0))
    return jnp.mod(summed, KGRID).astype(jnp.float32) * (2.0 * math.pi / KGRID)

def coupling(q_angle, eigvec, omega):
    mode_scale = 1.0 / jnp.sqrt(2.0 * omega)
    cos_phase = jnp.cos(q_angle)[:, None, None]
    sin_phase = jnp.sin(q_angle)[:, None, None]
    real_part = eigvec[0][None]
    imag_part = eigvec[1][None]
    coef_re = ((cos_phase * real_part - sin_phase * imag_part) * mode_scale).astype(jnp.bfloat16)
    coef_im = ((sin_phase * real_part + cos_phase * imag_part) * mode_scale).astype(jnp.bfloat16)
    return jnp.stack([jnp.stack([coef_re, coef_im], 2), jnp.stack([-coef_im, coef_re], 2)], 2)

def stacked(mode_block):
    row_count = mode_block.shape[0]
    vert_re = mode_block[:, :, 0, :].reshape(row_count, -1)
    vert_im = mode_block[:, :, 1, :].reshape(row_count, -1)
    upper = jnp.concatenate([vert_re, vert_im], 1)
    lower = jnp.concatenate([-vert_im, vert_re], 1)
    return jnp.concatenate([upper, lower], 0)

def pair_strength(bloch_sum, mode_count, normalizer):
    k_count = bloch_sum.shape[0]
    half_width = bloch_sum.shape[1] // 2
    bloch_re = bloch_sum[:, :half_width].reshape(k_count, mode_count, W, W)
    bloch_im = bloch_sum[:, half_width:].reshape(k_count, mode_count, W, W)
    summed = lax.optimization_barrier(jnp.sum(bloch_re * bloch_re + bloch_im * bloch_im, axis=3)) / normalizer
    return summed.transpose(1, 2, 0)

def reference(g_wan, el_cells, ph_cells, q_point, kpoints, eigvec, omega):
    q_angle = angles(q_point[:, None], ph_cells)[0]
    coupling_table = coupling(q_angle, eigvec, omega).astype(jnp.float32)

    def vertex_row(cell_row):
        return jnp.einsum('pncom,pncw->mow', coupling_table, cell_row.astype(jnp.float32))
    mode_vertex = lax.map(vertex_row, g_wan).astype(jnp.bfloat16)
    stacked_rows = stacked(mode_vertex)
    normalizer = float(NRE * NRP * W)
    k_blocks = kpoints.reshape(3, N_KA, K_DEV).transpose(1, 0, 2)

    def strength_block(k_numer):
        k_angle = angles(k_numer, el_cells)
        phase_left = jnp.concatenate([jnp.cos(k_angle), jnp.sin(k_angle)], 1).astype(jnp.bfloat16)
        bloch_sum = jnp.dot(phase_left, stacked_rows, preferred_element_type=jnp.float32)
        return pair_strength(bloch_sum, NU, normalizer)
    results = lax.map(strength_block, k_blocks)
    return results.transpose(1, 2, 0, 3).reshape(NU, W, NK)
```

```python
import math

import jax
import jax.numpy as jnp
from jax import lax
from jax.experimental import pallas as pl
from jax.experimental.pallas import tpu as pltpu
from jax.sharding import Mesh, PartitionSpec as P

W = 32
KGRID = 64
PH = ("xl", "core")
KA = ("xh", "z", "y")
SWAP = [(0, 1), (1, 0)]


def coupling(q_angle, eigvec, omega):
    mode_scale = 1.0 / jnp.sqrt(2.0 * omega)
    cos_phase = jnp.cos(q_angle)[:, None, None]
    sin_phase = jnp.sin(q_angle)[:, None, None]
    real_part = eigvec[0][None]
    imag_part = eigvec[1][None]
    coef_re = ((cos_phase * real_part - sin_phase * imag_part) * mode_scale).astype(jnp.bfloat16)
    coef_im = ((sin_phase * real_part + cos_phase * imag_part) * mode_scale).astype(jnp.bfloat16)
    return jnp.stack([jnp.stack([coef_re, coef_im], 2), jnp.stack([-coef_im, coef_re], 2)], 2)


def strength_kernel(modes, scale, kp_ref, el_ref, table_ref, vert_ref, out_ref, left, phase):
    cells = vert_ref.shape[0]
    width = kp_ref.shape[1]

    @pl.when(pl.program_id(0) == 0)
    def _():
        turned = vert_ref[...].astype(jnp.float32).T
        for m in range(modes):
            re = turned[m * 2 * W : m * 2 * W + W]
            im = turned[m * 2 * W + W : (m + 1) * 2 * W]
            rows = pl.ds(m * 2 * W, 2 * W)
            left[rows, :cells] = jnp.concatenate([re, im], 0).astype(jnp.bfloat16)
            left[rows, cells:] = jnp.concatenate([-im, re], 0).astype(jnp.bfloat16)

    numer = jnp.dot(el_ref[...], kp_ref[...], preferred_element_type=jnp.float32)
    index = numer.astype(jnp.int32) & 127
    for lane in range(0, width, 128):
        part = index[:, lane : lane + 128]
        cos_table = jnp.broadcast_to(table_ref[0:1, :], (cells, 128))
        sin_table = jnp.broadcast_to(table_ref[1:2, :], (cells, 128))
        cos = jnp.take_along_axis(cos_table, part, axis=1)
        sin = jnp.take_along_axis(sin_table, part, axis=1)
        phase[:cells, lane : lane + 128] = cos.astype(jnp.bfloat16)
        phase[cells:, lane : lane + 128] = sin.astype(jnp.bfloat16)
    bloch = jnp.dot(left[...], phase[...], preferred_element_type=jnp.float32)
    square = bloch * bloch
    total = jnp.sum(square.reshape(modes, 2 * W, width), axis=1) * scale
    for lane in range(0, width, 128):
        row = lane // 128 * modes
        out_ref[0, row : row + modes, :] = total[:, lane : lane + 128]


def strengths(kp, el, table, vert, modes, scale, dests):
    cells, cols = vert.shape
    width = kp.shape[1] // dests
    return pl.pallas_call(
        lambda *refs: strength_kernel(modes, scale, *refs),
        grid=(dests,),
        in_specs=[
            pl.BlockSpec((kp.shape[0], width), lambda i: (0, i)),
            pl.BlockSpec(el.shape, lambda i: (0, 0)),
            pl.BlockSpec(table.shape, lambda i: (0, 0)),
            pl.BlockSpec(vert.shape, lambda i: (0, 0)),
        ],
        out_specs=pl.BlockSpec((1, modes * width // 128, 128), lambda i: (i, 0, 0)),
        out_shape=jax.ShapeDtypeStruct((dests, modes * width // 128, 128), jnp.float32),
        scratch_shapes=[
            pltpu.VMEM((cols, 2 * cells), jnp.bfloat16),
            pltpu.VMEM((2 * cells, width), jnp.bfloat16),
        ],
        cost_estimate=pl.CostEstimate(
            flops=4 * cols * cells * kp.shape[1], bytes_accessed=2 * vert.size, transcendentals=0
        ),
        name="strengths",
    )(kp, el, table, vert)


def shards(g_wan, el_cells, ph_cells, q_point, kpoints, eigvec, omega):
    bf16, f32 = jnp.bfloat16, jnp.float32
    xl, core, xh = (lax.axis_index(a) for a in ("xl", "core", "xh"))
    e = g_wan.shape[0]
    k_dev = kpoints.shape[1]
    nu = eigvec.shape[1]
    modes = nu // 4
    unit = 2.0 * math.pi / KGRID
    q_sum = jnp.sum(q_point[:, None] * ph_cells, axis=0)
    q_angle = jnp.mod(q_sum, KGRID).astype(f32) * unit
    table = coupling(q_angle, eigvec, omega)
    partial = jnp.einsum("pncom,epncw->emow", table, g_wan, preferred_element_type=f32)
    partial = partial.reshape(e, 2, 2, modes, 2, W * W)
    mine = lax.dynamic_index_in_dim(partial, core, 2, keepdims=False)
    theirs = lax.dynamic_index_in_dim(partial, 1 - core, 2, keepdims=False)
    both = mine + lax.ppermute(theirs, "core", SWAP)
    mine = lax.dynamic_index_in_dim(both, xl, 1, keepdims=False)
    theirs = lax.dynamic_index_in_dim(both, 1 - xl, 1, keepdims=False).astype(bf16)
    vert = (mine + lax.ppermute(theirs, "xl", SWAP).astype(f32)).astype(bf16)
    vert = vert.reshape(e, 2 * modes, W, W).transpose(2, 0, 1, 3).reshape(W, -1, 128)
    kp = jnp.broadcast_to(kpoints.astype(bf16).reshape(1, -1, 128), (W, 3 * k_dev // 128, 128))
    rows = vert.shape[1]
    moved = lax.all_to_all(jnp.concatenate([vert, kp], 1), ("z", "y"), 0, 0, tiled=True)
    own = moved[:, :rows].reshape(W * e, 2 * modes * W)
    kp = moved[:, rows:].reshape(W, 3, k_dev).transpose(1, 0, 2).reshape(3, W * k_dev)
    other = lax.ppermute(own, "xh", SWAP)
    half = W * e
    el = el_cells.astype(bf16).T
    el = jnp.concatenate(
        [
            lax.dynamic_slice_in_dim(el, xh * half, half, 0),
            lax.dynamic_slice_in_dim(el, (1 - xh) * half, half, 0),
        ]
    )
    el = jnp.pad(el, ((0, 0), (0, 5)))
    kp = jnp.pad(kp, ((0, 5), (0, 0)))
    angle = (jnp.arange(128) % KGRID).astype(f32) * unit
    trig = jnp.stack([jnp.cos(angle), jnp.sin(angle)]).astype(bf16).astype(f32)
    trig = jnp.pad(trig, ((0, 6), (0, 0)))
    scale = 1.0 / float(el_cells.shape[1] * nu * W)
    found = strengths(kp, el, trig, jnp.concatenate([own, other]), modes, scale, W)
    found = lax.all_to_all(found, ("z", "y"), 0, 0, tiled=True)
    found = found.reshape(W, k_dev // 128, modes, 128).transpose(2, 0, 1, 3)
    return found.reshape(modes, W, k_dev)


def solution(mesh):
    split = Mesh(mesh.devices.reshape(2, 2, 2, 8, 4), PH + KA)
    return jax.shard_map(
        shards,
        mesh=split,
        in_specs=(
            P(KA, PH, None, None, None),
            P(),
            P(None, PH),
            P(),
            P(None, KA),
            P(),
            P(),
        ),
        out_specs=P(PH, None, KA),
        check_vma=False,
    )
```

```python
import math

import jax
import jax.numpy as jnp
from jax import lax
from jax.experimental import pallas as pl
from jax.experimental.pallas import tpu as pltpu
from jax.sharding import Mesh, PartitionSpec as P

W = 32
KGRID = 64
PH = ("xl", "core")
KA = ("xh", "z", "y")
SWAP = [(0, 1), (1, 0)]
CELLS = 128
K_STEP = 1024
K_BLOCK = 2048
EARLY = 6144
VMEM_MIB = 32


def coupling(q_angle, eigvec, omega):
    mode_scale = 1.0 / jnp.sqrt(2.0 * omega)
    cos_phase = jnp.cos(q_angle)[:, None, None]
    sin_phase = jnp.sin(q_angle)[:, None, None]
    real_part = eigvec[0][None]
    imag_part = eigvec[1][None]
    coef_re = ((cos_phase * real_part - sin_phase * imag_part) * mode_scale).astype(jnp.bfloat16)
    coef_im = ((sin_phase * real_part + cos_phase * imag_part) * mode_scale).astype(jnp.bfloat16)
    return jnp.stack([jnp.stack([coef_re, coef_im], 2), jnp.stack([-coef_im, coef_re], 2)], 2)


def fill_left(vert_ref, left, column):
    turned = vert_ref[...].astype(jnp.float32).T
    count = turned.shape[1]
    half = turned.shape[0] // 2
    left[:, column : column + count] = turned.astype(jnp.bfloat16)
    crossed = jnp.concatenate([-turned[half:], turned[:half]], 0)
    left[:, column + count : column + 2 * count] = crossed.astype(jnp.bfloat16)


def fill_phase(el_ref, kp_ref, trig_ref, phase, k_start, k_stop, run_start, run_stop):
    for k in range(k_start, k_stop, K_STEP):
        numer = lax.dot_general(
            el_ref[:, run_start * CELLS : run_stop * CELLS],
            kp_ref[:, k : k + K_STEP],
            (((0,), (0,)), ((), ())),
            preferred_element_type=jnp.float32,
        )
        index = numer.astype(jnp.int32) & 127
        for lane in range(0, K_STEP, 128):
            for run in range(numer.shape[0] // CELLS):
                part = index[run * CELLS : (run + 1) * CELLS, lane : lane + 128]
                for which in range(2):
                    values = jnp.broadcast_to(trig_ref[which : which + 1, :], part.shape)
                    found = jnp.take_along_axis(values, part, axis=1)
                    row = (2 * (run_start + run) + which) * CELLS
                    phase[row : row + CELLS, k + lane : k + lane + 128] = found.astype(jnp.bfloat16)


def own_kernel(vert_ref, kp_ref, el_ref, trig_ref, out_ref, left, phase):
    fill_left(vert_ref, left, 0)
    early = out_ref.shape[1]
    fill_phase(el_ref, kp_ref, trig_ref, phase, 0, early, 0, 1)
    for k in range(0, early, K_BLOCK):
        part = phase[: 2 * CELLS, k : k + K_BLOCK]
        out_ref[:, k : k + K_BLOCK] = jnp.dot(left[...], part, preferred_element_type=jnp.float32)


def strength_kernel(
    modes, scale, own_ref, other_ref, kp_ref, el_ref, trig_ref, sum_ref, out_ref, left, phase
):
    fill_left(own_ref, left, 0)
    fill_left(other_ref, left, 2 * CELLS)
    k_count = kp_ref.shape[1]
    early = sum_ref.shape[1]
    width = k_count // out_ref.shape[0]
    fill_phase(el_ref, kp_ref, trig_ref, phase, 0, early, 1, 2)
    fill_phase(el_ref, kp_ref, trig_ref, phase, early, k_count, 0, 2)
    for k in range(0, k_count, K_BLOCK):
        at = slice(k, k + K_BLOCK)
        if k < early:
            bloch = sum_ref[:, at] + jnp.dot(
                left[:, 2 * CELLS :], phase[2 * CELLS :, at], preferred_element_type=jnp.float32
            )
        else:
            bloch = jnp.dot(left[...], phase[:, at], preferred_element_type=jnp.float32)
        square = (bloch * bloch).reshape(2 * modes, W, K_BLOCK)
        total = jnp.sum(square[:modes] + square[modes:], axis=1) * scale
        for lane in range(0, K_BLOCK, 128):
            dest, row = divmod(k + lane, width)
            row = row // 128 * modes
            out_ref[dest, row : row + modes, :] = total[:, lane : lane + 128]


def strengths(own, other, kp, el, trig, modes, scale, dests):
    cells, cols = own.shape
    k_count = kp.shape[1]
    early = EARLY
    vmem = pl.BlockSpec(memory_space=pltpu.VMEM)
    params = pltpu.CompilerParams(vmem_limit_bytes=VMEM_MIB * 2**20)
    f32, bf16 = jnp.float32, jnp.bfloat16
    summed = pl.pallas_call(
        own_kernel,
        out_shape=pltpu.VMEM((cols, early), f32),
        in_specs=[vmem] * 4,
        out_specs=vmem,
        scratch_shapes=[
            pltpu.VMEM((cols, 2 * cells), bf16),
            pltpu.VMEM((2 * cells, early), bf16),
        ],
        compiler_params=params,
        cost_estimate=pl.CostEstimate(
            flops=4 * cols * cells * early, bytes_accessed=4 * cols * early, transcendentals=0
        ),
        name="own",
    )(own, kp, el, trig)
    return pl.pallas_call(
        lambda *refs: strength_kernel(modes, scale, *refs),
        out_shape=jax.ShapeDtypeStruct((dests, modes * k_count // dests // 128, 128), f32),
        in_specs=[vmem] * 6,
        out_specs=vmem,
        scratch_shapes=[
            pltpu.VMEM((cols, 4 * cells), bf16),
            pltpu.VMEM((4 * cells, k_count), bf16),
        ],
        compiler_params=params,
        cost_estimate=pl.CostEstimate(
            flops=8 * cols * cells * k_count, bytes_accessed=4 * cols * early, transcendentals=0
        ),
        name="strengths",
    )(own, other, kp, el, trig, summed)


def shards(g_wan, el_cells, ph_cells, q_point, kpoints, eigvec, omega):
    bf16, f32 = jnp.bfloat16, jnp.float32
    xl, core, xh = (lax.axis_index(a) for a in ("xl", "core", "xh"))
    e = g_wan.shape[0]
    k_dev = kpoints.shape[1]
    nu = eigvec.shape[1]
    modes = nu // 4
    unit = 2.0 * math.pi / KGRID
    q_sum = jnp.sum(q_point[:, None] * ph_cells, axis=0)
    q_angle = jnp.mod(q_sum, KGRID).astype(f32) * unit

    def reorder(x):
        lead = x.shape[:-1]
        return x.reshape(*lead, 2, 2, modes).swapaxes(-3, -2).reshape(*lead, nu)

    table = coupling(q_angle, reorder(eigvec), reorder(omega))
    partial = jnp.einsum("pncom,epncw->oemw", table, g_wan, preferred_element_type=f32)
    mine = lax.dynamic_slice_in_dim(partial, core * 2 * modes, 2 * modes, 2)
    theirs = lax.dynamic_slice_in_dim(partial, (1 - core) * 2 * modes, 2 * modes, 2)
    both = mine + lax.ppermute(theirs, "core", SWAP)
    mine = lax.dynamic_slice_in_dim(both, xl * modes, modes, 2)
    theirs = lax.dynamic_slice_in_dim(both, (1 - xl) * modes, modes, 2).astype(bf16)
    mine, theirs = mine.reshape(-1, W * W), theirs.reshape(-1, W * W)
    vert = (mine + lax.ppermute(theirs, "xl", SWAP).astype(f32)).astype(bf16)
    vert = vert.reshape(2, e, modes, W, W).transpose(3, 1, 0, 2, 4).reshape(W, -1, 128)
    kp = jnp.broadcast_to(kpoints.astype(bf16).reshape(1, -1, 128), (W, 3 * k_dev // 128, 128))
    rows = vert.shape[1]
    moved = lax.all_to_all(jnp.concatenate([vert, kp], 1), ("z", "y"), 0, 0, tiled=True)
    own = moved[:, :rows].reshape(W * e, 2 * modes * W)
    kp = moved[:, rows:].reshape(W, 3, k_dev).transpose(1, 0, 2).reshape(3, W * k_dev)
    other = lax.ppermute(own, "xh", SWAP)
    half = W * e
    el = el_cells.astype(bf16)
    el = jnp.concatenate(
        [
            lax.dynamic_slice_in_dim(el, xh * half, half, 1),
            lax.dynamic_slice_in_dim(el, (1 - xh) * half, half, 1),
        ],
        1,
    )
    el = jnp.pad(el, ((0, 5), (0, 0)))
    kp = jnp.pad(kp, ((0, 5), (0, 0)))
    angle = (jnp.arange(128) % KGRID).astype(f32) * unit
    trig = jnp.stack([jnp.cos(angle), jnp.sin(angle)]).astype(bf16).astype(f32)
    trig = jnp.pad(trig, ((0, 6), (0, 0)))
    scale = 1.0 / float(el_cells.shape[1] * nu * W)
    found = strengths(own, other, kp, el, trig, modes, scale, W)
    found = lax.all_to_all(found, ("z", "y"), 0, 0, tiled=True)
    found = found.reshape(W, k_dev // 128, modes, 128).transpose(2, 0, 1, 3)
    return found.reshape(modes, W, k_dev)


def solution(mesh):
    split = Mesh(mesh.devices.reshape(2, 2, 2, 8, 4), PH + KA)
    return jax.shard_map(
        shards,
        mesh=split,
        in_specs=(
            P(KA, PH, None, None, None),
            P(),
            P(None, PH),
            P(),
            P(None, KA),
            P(),
            P(),
        ),
        out_specs=P(PH, None, KA),
        check_vma=False,
    )
```

```python
import math

import jax
import jax.numpy as jnp
import numpy as np
from jax import lax
from jax.experimental import pallas as pl
from jax.experimental.pallas import tpu as pltpu
from jax.sharding import Mesh, PartitionSpec as P

W = 32
KGRID = 64
PH = ("xl", "core")
KA = ("xh", "z", "y")
SWAP = [(0, 1), (1, 0)]
CELLS = 128
K_STEP = 1024
K_BLOCK = 2048
EARLY = 6144
VMEM_MIB = 32
TRIO = 3
SENT = jnp.float16
ROOT_SCALE = 64.0


def row_table():
    rows = np.arange(2 * 2 * 4 * 2 * TRIO)
    trio, rest = rows % TRIO, rows // TRIO
    part, rest = rest % 2, rest // 2
    group, rest = rest % 4, rest // 4
    table = np.zeros((rows.size, 8), np.int32)
    table[:, 0] = group * TRIO + trio
    table[:, 1] = part
    table[:, 2] = rest % 2
    table[:, 3] = rest // 2
    return table


def trig_table(count):
    unit = np.float32(2.0 * math.pi / KGRID)
    angle = (np.arange(count) % KGRID).astype(np.float32) * unit
    return np.stack([np.cos(angle), np.sin(angle)]).astype(np.float32)


def fill_coupling(q_ref, cells_ref, trig_ref, eig_ref, omega_ref, rows_ref, table):
    nu = omega_ref.shape[1]
    count = rows_ref.shape[0]
    modes = nu // 4
    core, xl = lax.axis_index("core"), lax.axis_index("xl")
    at_core = jnp.where(rows_ref[:, 3:4] == 1, core, 1 - core)
    at_xl = jnp.where(rows_ref[:, 2:3] == 1, xl, 1 - xl)
    mode = rows_ref[:, 0:1] + (2 * at_xl + at_core) * modes
    pick = (lax.broadcasted_iota(jnp.int32, (count, nu), 1) == mode).astype(jnp.float32)
    inverse = 1.0 / jnp.sqrt(2.0 * omega_ref[...])
    scale = jnp.sum(pick * inverse, axis=1, keepdims=True)
    column = lax.broadcasted_iota(jnp.int32, (nu, 2 * nu), 1)
    twice = lax.broadcasted_iota(jnp.int32, (nu, 2 * nu), 0)
    spread = ((column == 2 * twice) | (column == 2 * twice + 1)).astype(jnp.float32)
    high = lax.Precision.HIGHEST
    planes = []
    for part in range(2):
        picked = lax.dot_general(
            pick, eig_ref[part], (((1,), (1,)), ((), ())),
            precision=high, preferred_element_type=jnp.float32,
        )
        planes.append(
            jnp.dot(picked, spread, precision=high, preferred_element_type=jnp.float32)
        )
    re, im = planes
    odd = (lax.broadcasted_iota(jnp.int32, (count, 2 * nu), 1) & 1) == 1
    lower = jnp.broadcast_to(rows_ref[:, 1:2], (count, 2 * nu)) == 1
    of_cos = jnp.where(lower, jnp.where(odd, re, im), jnp.where(odd, -im, re))
    of_sin = jnp.where(lower, jnp.where(odd, -im, re), jnp.where(odd, -re, -im))
    for p in range(cells_ref.shape[1]):
        turn = sum(q_ref[d] * cells_ref[d, p] for d in range(3)) & (KGRID - 1)
        value = (trig_ref[0, turn] * of_cos + trig_ref[1, turn] * of_sin) * scale
        table[:, p * 2 * nu : (p + 1) * 2 * nu] = value.astype(jnp.bfloat16)


def vertex_kernel(
    q_hbm, cells_hbm, trig_hbm, eig_hbm, omega_hbm, rows_hbm, g_ref, theirs_ref, mine_ref,
    q_ref, cells_ref, trig_ref, eig_ref, omega_ref, rows_ref, held, flat, table, small, sems,
):
    e_count, p_count, nu = g_ref.shape[:3]
    sources = (q_hbm, cells_hbm, trig_hbm, eig_hbm, omega_hbm, rows_hbm)
    targets = (q_ref, cells_ref, trig_ref, eig_ref, omega_ref, rows_ref)
    first = [
        pltpu.make_async_copy(source, target, small.at[i])
        for i, (source, target) in enumerate(zip(sources, targets))
    ]
    copies = [pltpu.make_async_copy(g_ref.at[e], held.at[e], sems.at[e]) for e in range(e_count)]
    for copy in first + copies:
        copy.start()
    for copy in first:
        copy.wait()
    fill_coupling(q_ref, cells_ref, trig_ref, eig_ref, omega_ref, rows_ref, table)
    part = 2 * TRIO

    def flatten(e):
        copies[e].wait()
        for p in range(p_count):
            flat[e % 2, p * 2 * nu : (p + 1) * 2 * nu, :] = held[e, p].reshape(2 * nu, W * W)

    flatten(0)
    for e in range(e_count):
        if e + 1 < e_count:
            flatten(e + 1)
        found = jnp.dot(table[...], flat[e % 2], preferred_element_type=jnp.float32)
        row = 0
        for out_ref in (theirs_ref, mine_ref):
            for side in range(2):
                for group in range(4):
                    to = (group * e_count + e) * part
                    out_ref[side, to : to + part, :] = found[row : row + part]
                    row += part


def partial_vertices(q_point, ph_cells, eigvec, omega, g_wan):
    e, p, nu = g_wan.shape[:3]
    rows = row_table()
    out = pltpu.VMEM((2, e * rows.shape[0] // 4, W * W), jnp.float32)
    vmem = pl.BlockSpec(memory_space=pltpu.VMEM)
    hbm = pl.BlockSpec(memory_space=pltpu.HBM)
    taken = [q_point, ph_cells, trig_table(KGRID), eigvec, omega.reshape(1, nu), rows, g_wan]
    taken = [pltpu.with_memory_space_constraint(jnp.asarray(x), pltpu.HBM) for x in taken]
    return pl.pallas_call(
        vertex_kernel,
        out_shape=(out, out),
        in_specs=[hbm] * 7,
        out_specs=(vmem, vmem),
        scratch_shapes=[
            pltpu.SMEM(q_point.shape, jnp.int32),
            pltpu.SMEM(ph_cells.shape, jnp.int32),
            pltpu.SMEM((2, KGRID), jnp.float32),
            pltpu.VMEM(eigvec.shape, jnp.float32),
            pltpu.VMEM((1, nu), jnp.float32),
            pltpu.VMEM(rows.shape, jnp.int32),
            pltpu.VMEM(g_wan.shape, g_wan.dtype),
            pltpu.VMEM((2, p * 2 * nu, W * W), jnp.bfloat16),
            pltpu.VMEM((rows.shape[0], p * 2 * nu), jnp.bfloat16),
            pltpu.SemaphoreType.DMA((6,)),
            pltpu.SemaphoreType.DMA((e,)),
        ],
        compiler_params=pltpu.CompilerParams(vmem_limit_bytes=40 * 2**20),
        cost_estimate=pl.CostEstimate(
            flops=2 * rows.shape[0] * g_wan.size, bytes_accessed=2 * g_wan.size, transcendentals=0
        ),
        name="vertices",
    )(*taken)


def fill_left(vert_ref, left, column):
    turned = vert_ref[...].astype(jnp.float32).T
    count = turned.shape[1]
    half = turned.shape[0] // 2
    left[:, column : column + count] = turned.astype(jnp.bfloat16)
    crossed = jnp.concatenate([-turned[half:], turned[:half]], 0)
    left[:, column + count : column + 2 * count] = crossed.astype(jnp.bfloat16)


def fill_phase(el_ref, kp_ref, trig_ref, phase, k_start, k_stop, run_start, run_stop):
    for k in range(k_start, k_stop, K_STEP):
        numer = lax.dot_general(
            el_ref[:, run_start * CELLS : run_stop * CELLS],
            kp_ref[:, k : k + K_STEP],
            (((0,), (0,)), ((), ())),
            preferred_element_type=jnp.float32,
        )
        index = numer.astype(jnp.int32) & 127
        for lane in range(0, K_STEP, 128):
            for run in range(numer.shape[0] // CELLS):
                part = index[run * CELLS : (run + 1) * CELLS, lane : lane + 128]
                for which in range(2):
                    values = jnp.broadcast_to(trig_ref[which : which + 1, :], part.shape)
                    found = jnp.take_along_axis(values, part, axis=1)
                    row = (2 * (run_start + run) + which) * CELLS
                    phase[row : row + CELLS, k + lane : k + lane + 128] = found.astype(jnp.bfloat16)


def own_kernel(vert_ref, kp_ref, el_ref, trig_ref, out_ref, left, phase):
    fill_left(vert_ref, left, 0)
    early = out_ref.shape[1]
    fill_phase(el_ref, kp_ref, trig_ref, phase, 0, early, 0, 1)
    for k in range(0, early, K_BLOCK):
        part = phase[: 2 * CELLS, k : k + K_BLOCK]
        out_ref[:, k : k + K_BLOCK] = jnp.dot(left[...], part, preferred_element_type=jnp.float32)


def strength_kernel(
    modes, scale, own_ref, other_ref, kp_ref, el_ref, trig_ref, sum_ref, out_ref, left, phase
):
    fill_left(own_ref, left, 0)
    fill_left(other_ref, left, 2 * CELLS)
    k_count = kp_ref.shape[1]
    early = sum_ref.shape[1]
    width = k_count // out_ref.shape[0]
    fill_phase(el_ref, kp_ref, trig_ref, phase, 0, early, 1, 2)
    fill_phase(el_ref, kp_ref, trig_ref, phase, early, k_count, 0, 2)
    for k in range(0, k_count, K_BLOCK):
        at = slice(k, k + K_BLOCK)
        if k < early:
            bloch = sum_ref[:, at] + jnp.dot(
                left[:, 2 * CELLS :], phase[2 * CELLS :, at], preferred_element_type=jnp.float32
            )
        else:
            bloch = jnp.dot(left[...], phase[:, at], preferred_element_type=jnp.float32)
        square = (bloch * bloch).reshape(2 * modes, W, K_BLOCK)
        total = jnp.sum(square[:modes] + square[modes:], axis=1) * scale
        for lane in range(0, K_BLOCK, 128):
            dest, row = divmod(k + lane, width)
            row = row // 128 * modes
            out_ref[dest, row : row + modes, :] = total[:, lane : lane + 128]


def strengths(own, other, kp, el, trig, modes, scale, dests):
    cells, cols = own.shape
    k_count = kp.shape[1]
    early = EARLY
    vmem = pl.BlockSpec(memory_space=pltpu.VMEM)
    params = pltpu.CompilerParams(vmem_limit_bytes=VMEM_MIB * 2**20)
    f32, bf16 = jnp.float32, jnp.bfloat16
    summed = pl.pallas_call(
        own_kernel,
        out_shape=pltpu.VMEM((cols, early), f32),
        in_specs=[vmem] * 4,
        out_specs=vmem,
        scratch_shapes=[
            pltpu.VMEM((cols, 2 * cells), bf16),
            pltpu.VMEM((2 * cells, early), bf16),
        ],
        compiler_params=params,
        cost_estimate=pl.CostEstimate(
            flops=4 * cols * cells * early, bytes_accessed=4 * cols * early, transcendentals=0
        ),
        name="own",
    )(own, kp, el, trig)
    return pl.pallas_call(
        lambda *refs: strength_kernel(modes, scale, *refs),
        out_shape=jax.ShapeDtypeStruct((dests, modes * k_count // dests // 128, 128), f32),
        in_specs=[vmem] * 6,
        out_specs=vmem,
        scratch_shapes=[
            pltpu.VMEM((cols, 4 * cells), bf16),
            pltpu.VMEM((4 * cells, k_count), bf16),
        ],
        compiler_params=params,
        cost_estimate=pl.CostEstimate(
            flops=8 * cols * cells * k_count, bytes_accessed=4 * cols * early, transcendentals=0
        ),
        name="strengths",
    )(own, other, kp, el, trig, summed)


def pack_kernel(mine_ref, core_ref, passed_ref, kp_ref, out_ref):
    lanes = kp_ref.shape[1]
    halves = [slice(lane, lane + 128) for lane in range(0, lanes, 128)]
    kp = jnp.concatenate([kp_ref[d : d + 1, at] for d in range(3) for at in halves])
    kp = kp.astype(jnp.float32).astype(jnp.bfloat16)
    rows = out_ref.shape[1] - kp.shape[0]
    total = mine_ref[1] + core_ref[1] + passed_ref[...].astype(jnp.float32)
    total = total.astype(jnp.bfloat16)
    for block in range(out_ref.shape[0]):
        lane, group = block // 4 * 128, block % 4 * rows
        out_ref[block, :rows, :] = total[group : group + rows, lane : lane + 128]
        out_ref[block, rows:, :] = kp


def pack(mine, core_part, passed, kp):
    rows = passed.shape[0] // 4 + kp.size // 128
    vmem = pl.BlockSpec(memory_space=pltpu.VMEM)
    return pl.pallas_call(
        pack_kernel,
        out_shape=jax.ShapeDtypeStruct((W, rows, 128), jnp.bfloat16),
        in_specs=[vmem] * 4,
        out_specs=vmem,
        compiler_params=pltpu.CompilerParams(vmem_limit_bytes=16 * 2**20),
        name="pack",
    )(mine, core_part, passed, kp)


def unpack_kernel(in_ref, out_ref):
    halves = out_ref.shape[2] // 128
    for block in range(in_ref.shape[0]):
        root = in_ref[block] * (1.0 / ROOT_SCALE)
        square = root * root
        value = square * square
        first, group = block // 4 * 4, block % 4 * TRIO
        for half in range(halves):
            for trio in range(TRIO):
                row = (half * TRIO + trio) * 4
                lanes = slice(half * 128, half * 128 + 128)
                out_ref[group + trio, first : first + 4, lanes] = value[row : row + 4]


def unpack(found, modes, k_dev):
    vmem = pl.BlockSpec(memory_space=pltpu.VMEM)
    return pl.pallas_call(
        unpack_kernel,
        out_shape=jax.ShapeDtypeStruct((modes, W, k_dev), jnp.float32),
        in_specs=[vmem],
        out_specs=vmem,
        compiler_params=pltpu.CompilerParams(vmem_limit_bytes=16 * 2**20),
        name="unpack",
    )(found)


def shards(g_wan, el_cells, ph_cells, q_point, kpoints, eigvec, omega):
    bf16, f32 = jnp.bfloat16, jnp.float32
    xh = lax.axis_index("xh")
    e = g_wan.shape[0]
    k_dev = kpoints.shape[1]
    nu = eigvec.shape[1]
    modes = nu // 4
    theirs, mine = partial_vertices(q_point, ph_cells, eigvec, omega, g_wan)
    core_part = lax.ppermute(theirs, "core", SWAP)
    passed = lax.ppermute((mine[0] + core_part[0]).astype(bf16), "xl", SWAP)
    sent = pack(mine, core_part, passed, kpoints)
    rows = passed.shape[0] // 4
    moved = lax.all_to_all(sent, ("z", "y"), 0, 0, tiled=True)
    own = moved[:, :rows].reshape(W * e, 2 * modes * W)
    kp = moved[:, rows:].reshape(W, 3, k_dev).transpose(1, 0, 2).reshape(3, W * k_dev)
    other = lax.ppermute(own, "xh", SWAP)
    half = W * e
    el = el_cells.astype(bf16)
    el = jnp.concatenate(
        [
            lax.dynamic_slice_in_dim(el, xh * half, half, 1),
            lax.dynamic_slice_in_dim(el, (1 - xh) * half, half, 1),
        ],
        1,
    )
    el = jnp.pad(el, ((0, 5), (0, 0)))
    kp = jnp.pad(kp, ((0, 5), (0, 0)))
    trig = np.pad(trig_table(128), ((0, 6), (0, 0)))
    scale = 1.0 / float(el_cells.shape[1] * nu * W)
    found = strengths(own, other, kp, el, trig, modes, scale, W)
    root = jnp.sqrt(jnp.sqrt(found)) * ROOT_SCALE
    found = lax.all_to_all(root.astype(SENT), ("z", "y"), 0, 0, tiled=True)
    return unpack(found.astype(f32), modes, k_dev)


def solution(mesh):
    split = Mesh(mesh.devices.reshape(2, 2, 2, 8, 4), PH + KA)
    return jax.shard_map(
        shards,
        mesh=split,
        in_specs=(
            P(KA, PH, None, None, None),
            P(),
            P(None, PH),
            P(),
            P(None, KA),
            P(),
            P(),
        ),
        out_specs=P(PH, None, KA),
        check_vma=False,
    )
```

```python
import math

import jax
import jax.numpy as jnp
import numpy as np
from jax import lax
from jax.experimental import pallas as pl
from jax.experimental.pallas import tpu as pltpu
from jax.sharding import Mesh, PartitionSpec as P

W = 32
KGRID = 64
PH = ("xl", "core")
KA = ("xh", "z", "y")
SWAP = [(0, 1), (1, 0)]
CELLS = 128
K_STEP = 1024
K_BLOCK = 1024
EARLY = 8192
VMEM_MIB = 26
TRIO = 3
SENT = jnp.float16
ROOT_SCALE = 64.0


def row_table():
    rows = np.arange(2 * 2 * 4 * 2 * TRIO)
    trio, rest = rows % TRIO, rows // TRIO
    part, rest = rest % 2, rest // 2
    group, rest = rest % 4, rest // 4
    table = np.zeros((rows.size, 8), np.int32)
    table[:, 0] = group * TRIO + trio
    table[:, 1] = part
    table[:, 2] = rest % 2
    table[:, 3] = rest // 2
    return table


def trig_table(count):
    unit = np.float32(2.0 * math.pi / KGRID)
    angle = (np.arange(count) % KGRID).astype(np.float32) * unit
    return np.stack([np.cos(angle), np.sin(angle)]).astype(np.float32)


def fill_coupling(q_ref, cells_ref, trig_ref, eig_ref, omega_ref, rows_ref, table):
    nu = omega_ref.shape[1]
    count = rows_ref.shape[0]
    modes = nu // 4
    core, xl = lax.axis_index("core"), lax.axis_index("xl")
    at_core = jnp.where(rows_ref[:, 3:4] == 1, core, 1 - core)
    at_xl = jnp.where(rows_ref[:, 2:3] == 1, xl, 1 - xl)
    mode = rows_ref[:, 0:1] + (2 * at_xl + at_core) * modes
    pick = (lax.broadcasted_iota(jnp.int32, (count, nu), 1) == mode).astype(jnp.float32)
    inverse = 1.0 / jnp.sqrt(2.0 * omega_ref[...])
    scale = jnp.sum(pick * inverse, axis=1, keepdims=True)
    column = lax.broadcasted_iota(jnp.int32, (nu, 2 * nu), 1)
    twice = lax.broadcasted_iota(jnp.int32, (nu, 2 * nu), 0)
    spread = ((column == 2 * twice) | (column == 2 * twice + 1)).astype(jnp.float32)
    high = lax.Precision.HIGHEST
    planes = []
    for part in range(2):
        picked = lax.dot_general(
            pick, eig_ref[part], (((1,), (1,)), ((), ())),
            precision=high, preferred_element_type=jnp.float32,
        )
        planes.append(
            jnp.dot(picked, spread, precision=high, preferred_element_type=jnp.float32)
        )
    re, im = planes
    odd = (lax.broadcasted_iota(jnp.int32, (count, 2 * nu), 1) & 1) == 1
    lower = jnp.broadcast_to(rows_ref[:, 1:2], (count, 2 * nu)) == 1
    of_cos = jnp.where(lower, jnp.where(odd, re, im), jnp.where(odd, -im, re))
    of_sin = jnp.where(lower, jnp.where(odd, -im, re), jnp.where(odd, -re, -im))
    for p in range(cells_ref.shape[1]):
        turn = sum(q_ref[d] * cells_ref[d, p] for d in range(3)) & (KGRID - 1)
        value = (trig_ref[0, turn] * of_cos + trig_ref[1, turn] * of_sin) * scale
        table[:, p * 2 * nu : (p + 1) * 2 * nu] = value.astype(jnp.bfloat16)


def vertex_kernel(
    q_hbm, cells_hbm, trig_hbm, eig_hbm, omega_hbm, rows_hbm, g_ref, theirs_ref, mine_ref,
    q_ref, cells_ref, trig_ref, eig_ref, omega_ref, rows_ref, held, flat, table, small, sems,
):
    e_count, p_count, nu = g_ref.shape[:3]
    sources = (q_hbm, cells_hbm, trig_hbm, eig_hbm, omega_hbm, rows_hbm)
    targets = (q_ref, cells_ref, trig_ref, eig_ref, omega_ref, rows_ref)
    first = [
        pltpu.make_async_copy(source, target, small.at[i])
        for i, (source, target) in enumerate(zip(sources, targets))
    ]
    copies = [pltpu.make_async_copy(g_ref.at[e], held.at[e], sems.at[e]) for e in range(e_count)]
    for copy in first + copies:
        copy.start()
    for copy in first:
        copy.wait()
    copies[0].wait()
    fill_coupling(q_ref, cells_ref, trig_ref, eig_ref, omega_ref, rows_ref, table)
    part = 2 * TRIO

    def flatten(e):
        for p in range(p_count):
            flat[e % 2, p * 2 * nu : (p + 1) * 2 * nu, :] = held[e, p].reshape(2 * nu, W * W)

    flatten(0)
    for e in range(e_count):
        if e + 1 < e_count:
            copies[e + 1].wait()
            flatten(e + 1)
        found = jnp.dot(table[...], flat[e % 2], preferred_element_type=jnp.float32)
        row = 0
        for out_ref in (theirs_ref, mine_ref):
            for side in range(2):
                for group in range(4):
                    to = (group * e_count + e) * part
                    out_ref[side, to : to + part, :] = found[row : row + part]
                    row += part


def partial_vertices(q_point, ph_cells, eigvec, omega, g_wan):
    e, p, nu = g_wan.shape[:3]
    rows = row_table()
    out = pltpu.VMEM((2, e * rows.shape[0] // 4, W * W), jnp.float32)
    vmem = pl.BlockSpec(memory_space=pltpu.VMEM)
    hbm = pl.BlockSpec(memory_space=pltpu.HBM)
    taken = [q_point, ph_cells, trig_table(KGRID), eigvec, omega.reshape(1, nu), rows, g_wan]
    taken = [pltpu.with_memory_space_constraint(jnp.asarray(x), pltpu.HBM) for x in taken]
    return pl.pallas_call(
        vertex_kernel,
        out_shape=(out, out),
        in_specs=[hbm] * 7,
        out_specs=(vmem, vmem),
        scratch_shapes=[
            pltpu.SMEM(q_point.shape, jnp.int32),
            pltpu.SMEM(ph_cells.shape, jnp.int32),
            pltpu.SMEM((2, KGRID), jnp.float32),
            pltpu.VMEM(eigvec.shape, jnp.float32),
            pltpu.VMEM((1, nu), jnp.float32),
            pltpu.VMEM(rows.shape, jnp.int32),
            pltpu.VMEM(g_wan.shape, g_wan.dtype),
            pltpu.VMEM((2, p * 2 * nu, W * W), jnp.bfloat16),
            pltpu.VMEM((rows.shape[0], p * 2 * nu), jnp.bfloat16),
            pltpu.SemaphoreType.DMA((6,)),
            pltpu.SemaphoreType.DMA((e,)),
        ],
        compiler_params=pltpu.CompilerParams(vmem_limit_bytes=40 * 2**20),
        cost_estimate=pl.CostEstimate(
            flops=2 * rows.shape[0] * g_wan.size, bytes_accessed=2 * g_wan.size, transcendentals=0
        ),
        name="vertices",
    )(*taken)


def fill_left(vert_ref, left, column):
    turned = vert_ref[...].astype(jnp.float32).T
    count = turned.shape[1]
    half = turned.shape[0] // 2
    left[:, column : column + count] = turned.astype(jnp.bfloat16)
    crossed = jnp.concatenate([-turned[half:], turned[:half]], 0)
    left[:, column + count : column + 2 * count] = crossed.astype(jnp.bfloat16)


def fill_phase(el_ref, kp_ref, trig_ref, phase, k_start, k_stop, run_start, run_stop):
    for k in range(k_start, k_stop, K_STEP):
        numer = lax.dot_general(
            el_ref[:, run_start * CELLS : run_stop * CELLS],
            kp_ref[:, k : k + K_STEP],
            (((0,), (0,)), ((), ())),
            preferred_element_type=jnp.float32,
        )
        index = numer.astype(jnp.int32) & 127
        for lane in range(0, K_STEP, 128):
            for run in range(numer.shape[0] // CELLS):
                part = index[run * CELLS : (run + 1) * CELLS, lane : lane + 128]
                for which in range(2):
                    values = jnp.broadcast_to(trig_ref[which : which + 1, :], part.shape)
                    found = jnp.take_along_axis(values, part, axis=1)
                    row = (2 * (run_start + run) + which) * CELLS
                    phase[row : row + CELLS, k + lane : k + lane + 128] = found.astype(jnp.bfloat16)


def own_kernel(vert_ref, kp_ref, el_ref, trig_ref, out_ref, left, phase):
    fill_left(vert_ref, left, 0)
    early = out_ref.shape[1]
    fill_phase(el_ref, kp_ref, trig_ref, phase, 0, early, 0, 1)
    for k in range(0, early, K_BLOCK):
        part = phase[: 2 * CELLS, k : k + K_BLOCK]
        out_ref[:, k : k + K_BLOCK] = jnp.dot(left[...], part, preferred_element_type=jnp.float32)


def strength_kernel(
    modes, scale, own_ref, other_ref, kp_ref, el_ref, trig_ref, sum_ref, out_ref, left, phase
):
    fill_left(own_ref, left, 0)
    fill_left(other_ref, left, 2 * CELLS)
    k_count = kp_ref.shape[1]
    early = sum_ref.shape[1]
    width = k_count // out_ref.shape[0]
    fill_phase(el_ref, kp_ref, trig_ref, phase, 0, early, 1, 2)
    fill_phase(el_ref, kp_ref, trig_ref, phase, early, k_count, 0, 2)
    for k in range(0, k_count, K_BLOCK):
        at = slice(k, k + K_BLOCK)
        if k < early:
            bloch = sum_ref[:, at] + jnp.dot(
                left[:, 2 * CELLS :], phase[2 * CELLS :, at], preferred_element_type=jnp.float32
            )
        else:
            bloch = jnp.dot(left[...], phase[:, at], preferred_element_type=jnp.float32)
        square = (bloch * bloch).reshape(2 * modes, W, K_BLOCK)
        total = jnp.sum(square[:modes] + square[modes:], axis=1) * scale
        for lane in range(0, K_BLOCK, 128):
            dest, row = divmod(k + lane, width)
            row = row // 128 * modes
            out_ref[dest, row : row + modes, :] = total[:, lane : lane + 128]


def strengths(own, other, kp, el, trig, modes, scale, dests):
    cells, cols = own.shape
    k_count = kp.shape[1]
    early = EARLY
    vmem = pl.BlockSpec(memory_space=pltpu.VMEM)
    params = pltpu.CompilerParams(vmem_limit_bytes=VMEM_MIB * 2**20)
    f32, bf16 = jnp.float32, jnp.bfloat16
    summed = pl.pallas_call(
        own_kernel,
        out_shape=pltpu.VMEM((cols, early), f32),
        in_specs=[vmem] * 4,
        out_specs=vmem,
        scratch_shapes=[
            pltpu.VMEM((cols, 2 * cells), bf16),
            pltpu.VMEM((2 * cells, early), bf16),
        ],
        compiler_params=params,
        cost_estimate=pl.CostEstimate(
            flops=4 * cols * cells * early, bytes_accessed=4 * cols * early, transcendentals=0
        ),
        name="own",
    )(own, kp, el, trig)
    return pl.pallas_call(
        lambda *refs: strength_kernel(modes, scale, *refs),
        out_shape=jax.ShapeDtypeStruct((dests, modes * k_count // dests // 128, 128), f32),
        in_specs=[vmem] * 6,
        out_specs=vmem,
        scratch_shapes=[
            pltpu.VMEM((cols, 4 * cells), bf16),
            pltpu.VMEM((4 * cells, k_count), bf16),
        ],
        compiler_params=params,
        cost_estimate=pl.CostEstimate(
            flops=8 * cols * cells * k_count, bytes_accessed=4 * cols * early, transcendentals=0
        ),
        name="strengths",
    )(own, other, kp, el, trig, summed)


def pack_kernel(mine_ref, core_ref, passed_ref, kp_ref, out_ref):
    lanes = kp_ref.shape[1]
    halves = [slice(lane, lane + 128) for lane in range(0, lanes, 128)]
    kp = jnp.concatenate([kp_ref[d : d + 1, at] for d in range(3) for at in halves])
    rows = out_ref.shape[1] - kp.shape[0]
    total = mine_ref[1] + core_ref[1] + passed_ref[...].astype(jnp.float32)
    total = total.astype(jnp.bfloat16)
    for block in range(out_ref.shape[0]):
        lane, group = block // 4 * 128, block % 4 * rows
        out_ref[block, :rows, :] = total[group : group + rows, lane : lane + 128]
        out_ref[block, rows:, :] = kp


def pack(mine, core_part, passed, kp):
    rows = passed.shape[0] // 4 + kp.size // 128
    vmem = pl.BlockSpec(memory_space=pltpu.VMEM)
    return pl.pallas_call(
        pack_kernel,
        out_shape=pltpu.VMEM((W, rows, 128), jnp.bfloat16),
        in_specs=[vmem] * 4,
        out_specs=vmem,
        compiler_params=pltpu.CompilerParams(vmem_limit_bytes=16 * 2**20),
        name="pack",
    )(mine, core_part, passed, kp)


def unpack_kernel(in_ref, out_ref):
    halves = out_ref.shape[2] // 128
    for block in range(in_ref.shape[0]):
        root = in_ref[block] * (1.0 / ROOT_SCALE)
        square = root * root
        value = square * square
        first, group = block // 4 * 4, block % 4 * TRIO
        for half in range(halves):
            for trio in range(TRIO):
                row = (half * TRIO + trio) * 4
                lanes = slice(half * 128, half * 128 + 128)
                out_ref[group + trio, first : first + 4, lanes] = value[row : row + 4]


def unpack(found, modes, k_dev):
    vmem = pl.BlockSpec(memory_space=pltpu.VMEM)
    return pl.pallas_call(
        unpack_kernel,
        out_shape=jax.ShapeDtypeStruct((modes, W, k_dev), jnp.float32),
        in_specs=[vmem],
        out_specs=vmem,
        compiler_params=pltpu.CompilerParams(vmem_limit_bytes=16 * 2**20),
        name="unpack",
    )(found)


def shards(g_wan, el_cells, ph_cells, q_point, kpoints, eigvec, omega):
    bf16, f32 = jnp.bfloat16, jnp.float32
    xh = lax.axis_index("xh")
    e = g_wan.shape[0]
    k_dev = kpoints.shape[1]
    nu = eigvec.shape[1]
    modes = nu // 4
    theirs, mine = partial_vertices(q_point, ph_cells, eigvec, omega, g_wan)
    core_part = lax.ppermute(theirs, "core", SWAP)
    passed = lax.ppermute((mine[0] + core_part[0]).astype(bf16), "xl", SWAP)
    sent = pack(mine, core_part, passed, kpoints.astype(bf16))
    rows = passed.shape[0] // 4
    moved = lax.all_to_all(sent, ("z", "y"), 0, 0, tiled=True)
    own = moved[:, :rows].reshape(W * e, 2 * modes * W)
    kp = moved[:, rows:].reshape(W, 3, k_dev).transpose(1, 0, 2).reshape(3, W * k_dev)
    other = lax.ppermute(own, "xh", SWAP)
    half = W * e
    el = el_cells.astype(bf16)
    el = jnp.concatenate(
        [
            lax.dynamic_slice_in_dim(el, xh * half, half, 1),
            lax.dynamic_slice_in_dim(el, (1 - xh) * half, half, 1),
        ],
        1,
    )
    el = jnp.pad(el, ((0, 5), (0, 0)))
    kp = jnp.pad(kp, ((0, 5), (0, 0)))
    angle = (jnp.arange(128) % KGRID).astype(f32) * (2.0 * math.pi / KGRID)
    trig = jnp.pad(jnp.stack([jnp.cos(angle), jnp.sin(angle)]), ((0, 6), (0, 0)))
    scale = 1.0 / float(el_cells.shape[1] * nu * W)
    found = strengths(own, other, kp, el, trig, modes, scale, W)
    root = jnp.sqrt(jnp.sqrt(found)) * ROOT_SCALE
    found = lax.all_to_all(root.astype(SENT), ("z", "y"), 0, 0, tiled=True)
    return unpack(found.astype(f32), modes, k_dev)


def solution(mesh):
    split = Mesh(mesh.devices.reshape(2, 2, 2, 8, 4), PH + KA)
    return jax.shard_map(
        shards,
        mesh=split,
        in_specs=(
            P(KA, PH, None, None, None),
            P(),
            P(None, PH),
            P(),
            P(None, KA),
            P(),
            P(),
        ),
        out_specs=P(PH, None, KA),
        check_vma=False,
    )
```

```python
import math

import jax
import jax.numpy as jnp
import numpy as np
from jax import lax
from jax.experimental import pallas as pl
from jax.experimental.pallas import tpu as pltpu
from jax.sharding import Mesh, PartitionSpec as P

W = 32
KGRID = 64
PH = ("xl", "core")
KA = ("xh", "z", "y")
SWAP = [(0, 1), (1, 0)]
CELLS = 128
K_STEP = 1024
K_BLOCK = 2048
EARLY = 8192
VMEM_MIB = 26
TRIO = 3
PIECES = 3
SENT = jnp.float16
ROOT_SCALE = 64.0


def row_table():
    rows = np.arange(2 * 2 * 4 * 2 * TRIO)
    trio, rest = rows % TRIO, rows // TRIO
    part, rest = rest % 2, rest // 2
    group, rest = rest % 4, rest // 4
    table = np.zeros((rows.size, 8), np.int32)
    table[:, 0] = group * TRIO + trio
    table[:, 1] = part
    table[:, 2] = rest % 2
    table[:, 3] = rest // 2
    return table


def trig_table(count):
    unit = np.float32(2.0 * math.pi / KGRID)
    angle = (np.arange(count) % KGRID).astype(np.float32) * unit
    return np.stack([np.cos(angle), np.sin(angle)]).astype(np.float32)


def fill_coupling(q_ref, cells_ref, trig_ref, eig_ref, omega_ref, rows_ref, table):
    nu = omega_ref.shape[1]
    count = rows_ref.shape[0]
    modes = nu // 4
    core, xl = lax.axis_index("core"), lax.axis_index("xl")
    at_core = jnp.where(rows_ref[:, 3:4] == 1, core, 1 - core)
    at_xl = jnp.where(rows_ref[:, 2:3] == 1, xl, 1 - xl)
    mode = rows_ref[:, 0:1] + (2 * at_xl + at_core) * modes
    pick = (lax.broadcasted_iota(jnp.int32, (count, nu), 1) == mode).astype(jnp.float32)
    inverse = 1.0 / jnp.sqrt(2.0 * omega_ref[...])
    scale = jnp.sum(pick * inverse, axis=1, keepdims=True)
    column = lax.broadcasted_iota(jnp.int32, (nu, 2 * nu), 1)
    twice = lax.broadcasted_iota(jnp.int32, (nu, 2 * nu), 0)
    spread = ((column == 2 * twice) | (column == 2 * twice + 1)).astype(jnp.float32)
    high = lax.Precision.HIGHEST
    planes = []
    for part in range(2):
        picked = lax.dot_general(
            pick, eig_ref[part], (((1,), (1,)), ((), ())),
            precision=high, preferred_element_type=jnp.float32,
        )
        planes.append(
            jnp.dot(picked, spread, precision=high, preferred_element_type=jnp.float32)
        )
    re, im = planes
    odd = (lax.broadcasted_iota(jnp.int32, (count, 2 * nu), 1) & 1) == 1
    lower = jnp.broadcast_to(rows_ref[:, 1:2], (count, 2 * nu)) == 1
    of_cos = jnp.where(lower, jnp.where(odd, re, im), jnp.where(odd, -im, re))
    of_sin = jnp.where(lower, jnp.where(odd, -im, re), jnp.where(odd, -re, -im))
    for p in range(cells_ref.shape[1]):
        turn = sum(q_ref[d] * cells_ref[d, p] for d in range(3)) & (KGRID - 1)
        value = (trig_ref[0, turn] * of_cos + trig_ref[1, turn] * of_sin) * scale
        table[:, p * 2 * nu : (p + 1) * 2 * nu] = value.astype(jnp.bfloat16)


def vertex_kernel(
    q_hbm, cells_hbm, trig_hbm, eig_hbm, omega_hbm, rows_hbm, g_ref, theirs_ref, mine_ref,
    q_ref, cells_ref, trig_ref, eig_ref, omega_ref, rows_ref, held, flat, table, small, sems,
):
    e_count, p_count, nu = g_ref.shape[:3]
    sources = (q_hbm, cells_hbm, trig_hbm, eig_hbm, omega_hbm, rows_hbm)
    targets = (q_ref, cells_ref, trig_ref, eig_ref, omega_ref, rows_ref)
    first = [
        pltpu.make_async_copy(source, target, small.at[i])
        for i, (source, target) in enumerate(zip(sources, targets))
    ]
    cut = p_count // PIECES
    copies = [
        [
            pltpu.make_async_copy(
                g_ref.at[e, pl.ds(piece * cut, cut)],
                held.at[e, pl.ds(piece * cut, cut)],
                sems.at[e, piece],
            )
            for piece in range(PIECES)
        ]
        for e in range(e_count)
    ]
    for copy in first + sum(copies, []):
        copy.start()
    for copy in first:
        copy.wait()
    for copy in copies[0]:
        copy.wait()
    fill_coupling(q_ref, cells_ref, trig_ref, eig_ref, omega_ref, rows_ref, table)
    part = 2 * TRIO

    def flatten(e):
        for p in range(p_count):
            flat[e % 2, p * 2 * nu : (p + 1) * 2 * nu, :] = held[e, p].reshape(2 * nu, W * W)

    flatten(0)
    for e in range(e_count):
        if e + 1 < e_count:
            for copy in copies[e + 1]:
                copy.wait()
            flatten(e + 1)
        found = jnp.dot(table[...], flat[e % 2], preferred_element_type=jnp.float32)
        row = 0
        for out_ref in (theirs_ref, mine_ref):
            for side in range(2):
                for group in range(4):
                    to = (group * e_count + e) * part
                    out_ref[side, to : to + part, :] = found[row : row + part]
                    row += part


def partial_vertices(q_point, ph_cells, eigvec, omega, g_wan):
    e, p, nu = g_wan.shape[:3]
    rows = row_table()
    out = pltpu.VMEM((2, e * rows.shape[0] // 4, W * W), jnp.float32)
    vmem = pl.BlockSpec(memory_space=pltpu.VMEM)
    hbm = pl.BlockSpec(memory_space=pltpu.HBM)
    taken = [q_point, ph_cells, trig_table(KGRID), eigvec, omega.reshape(1, nu), rows, g_wan]
    taken = [pltpu.with_memory_space_constraint(jnp.asarray(x), pltpu.HBM) for x in taken]
    return pl.pallas_call(
        vertex_kernel,
        out_shape=(out, out),
        in_specs=[hbm] * 7,
        out_specs=(vmem, vmem),
        scratch_shapes=[
            pltpu.SMEM(q_point.shape, jnp.int32),
            pltpu.SMEM(ph_cells.shape, jnp.int32),
            pltpu.SMEM((2, KGRID), jnp.float32),
            pltpu.VMEM(eigvec.shape, jnp.float32),
            pltpu.VMEM((1, nu), jnp.float32),
            pltpu.VMEM(rows.shape, jnp.int32),
            pltpu.VMEM(g_wan.shape, g_wan.dtype),
            pltpu.VMEM((2, p * 2 * nu, W * W), jnp.bfloat16),
            pltpu.VMEM((rows.shape[0], p * 2 * nu), jnp.bfloat16),
            pltpu.SemaphoreType.DMA((6,)),
            pltpu.SemaphoreType.DMA((e, PIECES)),
        ],
        compiler_params=pltpu.CompilerParams(vmem_limit_bytes=40 * 2**20),
        cost_estimate=pl.CostEstimate(
            flops=2 * rows.shape[0] * g_wan.size, bytes_accessed=2 * g_wan.size, transcendentals=0
        ),
        name="vertices",
    )(*taken)


def fill_left(vert_ref, left, column):
    turned = vert_ref[...].astype(jnp.float32).T
    count = turned.shape[1]
    half = turned.shape[0] // 2
    left[:, column : column + count] = turned.astype(jnp.bfloat16)
    crossed = jnp.concatenate([-turned[half:], turned[:half]], 0)
    left[:, column + count : column + 2 * count] = crossed.astype(jnp.bfloat16)


def fill_phase(el_ref, kp_ref, trig_ref, phase, k_start, k_stop, run_start, run_stop):
    for k in range(k_start, k_stop, K_STEP):
        numer = lax.dot_general(
            el_ref[:, run_start * CELLS : run_stop * CELLS],
            kp_ref[:, k : k + K_STEP],
            (((0,), (0,)), ((), ())),
            preferred_element_type=jnp.float32,
        )
        index = numer.astype(jnp.int32) & 127
        for lane in range(0, K_STEP, 128):
            for run in range(numer.shape[0] // CELLS):
                part = index[run * CELLS : (run + 1) * CELLS, lane : lane + 128]
                for which in range(2):
                    values = jnp.broadcast_to(trig_ref[which : which + 1, :], part.shape)
                    found = jnp.take_along_axis(values, part, axis=1)
                    row = (2 * (run_start + run) + which) * CELLS
                    phase[row : row + CELLS, k + lane : k + lane + 128] = found.astype(jnp.bfloat16)


def own_kernel(vert_ref, kp_ref, el_ref, trig_ref, out_ref, left, phase):
    fill_left(vert_ref, left, 0)
    early = out_ref.shape[1]
    fill_phase(el_ref, kp_ref, trig_ref, phase, 0, early, 0, 1)
    for k in range(0, early, K_BLOCK):
        part = phase[: 2 * CELLS, k : k + K_BLOCK]
        out_ref[:, k : k + K_BLOCK] = jnp.dot(left[...], part, preferred_element_type=jnp.float32)


def strength_kernel(
    modes, scale, own_ref, other_ref, kp_ref, el_ref, trig_ref, sum_ref, out_ref, left, phase
):
    fill_left(own_ref, left, 0)
    fill_left(other_ref, left, 2 * CELLS)
    k_count = kp_ref.shape[1]
    early = sum_ref.shape[1]
    width = k_count // out_ref.shape[0]
    fill_phase(el_ref, kp_ref, trig_ref, phase, 0, early, 1, 2)
    fill_phase(el_ref, kp_ref, trig_ref, phase, early, k_count, 0, 2)
    for k in range(0, k_count, K_BLOCK):
        at = slice(k, k + K_BLOCK)
        if k < early:
            bloch = sum_ref[:, at] + jnp.dot(
                left[:, 2 * CELLS :], phase[2 * CELLS :, at], preferred_element_type=jnp.float32
            )
        else:
            bloch = jnp.dot(left[...], phase[:, at], preferred_element_type=jnp.float32)
        square = (bloch * bloch).reshape(2 * modes, W, K_BLOCK)
        total = jnp.sum(square[:modes] + square[modes:], axis=1) * scale
        for lane in range(0, K_BLOCK, 128):
            dest, row = divmod(k + lane, width)
            row = row // 128 * modes
            out_ref[dest, row : row + modes, :] = total[:, lane : lane + 128]


def strengths(own, other, kp, el, trig, modes, scale, dests):
    cells, cols = own.shape
    k_count = kp.shape[1]
    early = EARLY
    vmem = pl.BlockSpec(memory_space=pltpu.VMEM)
    params = pltpu.CompilerParams(vmem_limit_bytes=VMEM_MIB * 2**20)
    f32, bf16 = jnp.float32, jnp.bfloat16
    summed = pl.pallas_call(
        own_kernel,
        out_shape=pltpu.VMEM((cols, early), f32),
        in_specs=[vmem] * 4,
        out_specs=vmem,
        scratch_shapes=[
            pltpu.VMEM((cols, 2 * cells), bf16),
            pltpu.VMEM((2 * cells, early), bf16),
        ],
        compiler_params=params,
        cost_estimate=pl.CostEstimate(
            flops=4 * cols * cells * early, bytes_accessed=4 * cols * early, transcendentals=0
        ),
        name="own",
    )(own, kp, el, trig)
    return pl.pallas_call(
        lambda *refs: strength_kernel(modes, scale, *refs),
        out_shape=jax.ShapeDtypeStruct((dests, modes * k_count // dests // 128, 128), f32),
        in_specs=[vmem] * 6,
        out_specs=vmem,
        scratch_shapes=[
            pltpu.VMEM((cols, 4 * cells), bf16),
            pltpu.VMEM((4 * cells, k_count), bf16),
        ],
        compiler_params=params,
        cost_estimate=pl.CostEstimate(
            flops=8 * cols * cells * k_count, bytes_accessed=4 * cols * early, transcendentals=0
        ),
        name="strengths",
    )(own, other, kp, el, trig, summed)


def pack_kernel(mine_ref, core_ref, passed_ref, kp_ref, out_ref):
    lanes = kp_ref.shape[1]
    halves = [slice(lane, lane + 128) for lane in range(0, lanes, 128)]
    kp = jnp.concatenate([kp_ref[d : d + 1, at] for d in range(3) for at in halves])
    rows = out_ref.shape[1] - kp.shape[0]
    total = mine_ref[1] + core_ref[1] + passed_ref[...].astype(jnp.float32)
    total = total.astype(jnp.bfloat16)
    for block in range(out_ref.shape[0]):
        lane, group = block // 4 * 128, block % 4 * rows
        out_ref[block, :rows, :] = total[group : group + rows, lane : lane + 128]
        out_ref[block, rows:, :] = kp


def pack(mine, core_part, passed, kp):
    rows = passed.shape[0] // 4 + kp.size // 128
    vmem = pl.BlockSpec(memory_space=pltpu.VMEM)
    return pl.pallas_call(
        pack_kernel,
        out_shape=pltpu.VMEM((W, rows, 128), jnp.bfloat16),
        in_specs=[vmem] * 4,
        out_specs=vmem,
        compiler_params=pltpu.CompilerParams(vmem_limit_bytes=16 * 2**20),
        name="pack",
    )(mine, core_part, passed, kp)


def unpack_kernel(in_ref, out_ref):
    halves = out_ref.shape[2] // 128
    for block in range(in_ref.shape[0]):
        root = in_ref[block] * (1.0 / ROOT_SCALE)
        square = root * root
        value = square * square
        first, group = block // 4 * 4, block % 4 * TRIO
        for half in range(halves):
            for trio in range(TRIO):
                row = (half * TRIO + trio) * 4
                lanes = slice(half * 128, half * 128 + 128)
                out_ref[group + trio, first : first + 4, lanes] = value[row : row + 4]


def unpack(found, modes, k_dev):
    vmem = pl.BlockSpec(memory_space=pltpu.VMEM)
    return pl.pallas_call(
        unpack_kernel,
        out_shape=jax.ShapeDtypeStruct((modes, W, k_dev), jnp.float32),
        in_specs=[vmem],
        out_specs=vmem,
        compiler_params=pltpu.CompilerParams(vmem_limit_bytes=16 * 2**20),
        name="unpack",
    )(found)


def shards(g_wan, el_cells, ph_cells, q_point, kpoints, eigvec, omega):
    bf16, f32 = jnp.bfloat16, jnp.float32
    xh = lax.axis_index("xh")
    e = g_wan.shape[0]
    k_dev = kpoints.shape[1]
    nu = eigvec.shape[1]
    modes = nu // 4
    theirs, mine = partial_vertices(q_point, ph_cells, eigvec, omega, g_wan)
    core_part = lax.ppermute(theirs, "core", SWAP)
    passed = lax.ppermute((mine[0] + core_part[0]).astype(bf16), "xl", SWAP)
    sent = pack(mine, core_part, passed, kpoints.astype(bf16))
    rows = passed.shape[0] // 4
    moved = lax.all_to_all(sent, ("z", "y"), 0, 0, tiled=True)
    own = moved[:, :rows].reshape(W * e, 2 * modes * W)
    kp = moved[:, rows:].reshape(W, 3, k_dev).transpose(1, 0, 2).reshape(3, W * k_dev)
    other = lax.ppermute(own, "xh", SWAP)
    half = W * e
    el = el_cells.astype(bf16)
    el = jnp.concatenate(
        [
            lax.dynamic_slice_in_dim(el, xh * half, half, 1),
            lax.dynamic_slice_in_dim(el, (1 - xh) * half, half, 1),
        ],
        1,
    )
    el = jnp.pad(el, ((0, 5), (0, 0)))
    kp = jnp.pad(kp, ((0, 5), (0, 0)))
    angle = (jnp.arange(128) % KGRID).astype(f32) * (2.0 * math.pi / KGRID)
    trig = jnp.pad(jnp.stack([jnp.cos(angle), jnp.sin(angle)]), ((0, 6), (0, 0)))
    scale = 1.0 / float(el_cells.shape[1] * nu * W)
    found = strengths(own, other, kp, el, trig, modes, scale, W)
    root = jnp.sqrt(jnp.sqrt(found)) * ROOT_SCALE
    found = lax.all_to_all(root.astype(SENT), ("z", "y"), 0, 0, tiled=True)
    return unpack(found.astype(f32), modes, k_dev)


def solution(mesh):
    split = Mesh(mesh.devices.reshape(2, 2, 2, 8, 4), PH + KA)
    return jax.shard_map(
        shards,
        mesh=split,
        in_specs=(
            P(KA, PH, None, None, None),
            P(),
            P(None, PH),
            P(),
            P(None, KA),
            P(),
            P(),
        ),
        out_specs=P(PH, None, KA),
        check_vma=False,
    )
```
